32 devices in a mesh: dp: 2 (over x), expert: 4 (over z), tensor: 4 (over y, core).
Axes of the slice: x: 2, y: 2, z: 4, core: 2. Of those that a mesh axis runs over, the one named last changes fastest.
Arguments:
- inputs: bfloat16 [32, 197, 768], P(('dp', 'expert')), may hold values from -6 to 6
- first_gain: bfloat16 [768], replicated, may hold values from 0.5 to 1.5
- first_shift: bfloat16 [768], replicated, may hold values from -3 to 3
- heads_weight: bfloat16 [768, 2304], P(None, 'tensor'), may hold values from -0.21875 to 0.21875
- heads_bias: bfloat16 [12, 128], P('tensor'), may hold values from -3 to 3
- merge_weight: bfloat16 [768, 768], P('tensor'), may hold values from -0.875 to 0.875
- merge_bias: bfloat16 [768], replicated, may hold values from -3 to 3
- second_gain: bfloat16 [768], replicated, may hold values from 0.5 to 1.5
- second_shift: bfloat16 [768], replicated, may hold values from -3 to 3
- router_weight: bfloat16 [768, 4], replicated, may hold values from -0.3125 to 0.3125
- expand_weight: bfloat16 [4, 768, 3072], P('expert', None, 'tensor'), may hold values from -0.21875 to 0.21875
- expand_bias: bfloat16 [4, 3072], P('expert', 'tensor'), may hold values from -3 to 3
- shrink_weight: bfloat16 [4, 3072, 768], P('expert', 'tensor'), may hold values from -0.4375 to 0.4375
- shrink_bias: bfloat16 [4, 768], P('expert'), may hold values from -4 to 4
- cotangent: bfloat16 [32, 197, 768], P(('dp', 'expert')), may hold values from -6 to 6
- expert_choice: int32 [32, 197, 2], P(('dp', 'expert')), may hold values from 0 to 3, as said below
- slot_index: int32 [32, 197, 2], P(('dp', 'expert')), may hold values from 0 to 391, as said below
- dropped: int32 [32, 197, 2], P(('dp', 'expert')), may hold values from 0 to 1, as said below
Outputs:
- outputs: bfloat16 [32, 197, 768], P(('dp', 'expert'))
- input_gradient: float32 [32, 197, 768], P(('dp', 'expert'))
- first_gain_gradient: float32 [768], replicated
- first_shift_gradient: float32 [768], replicated
- heads_weight_gradient: float32 [768, 2304], P(None, 'tensor')
- heads_bias_gradient: float32 [12, 128], P('tensor')
- merge_weight_gradient: float32 [768, 768], P('tensor')
- merge_bias_gradient: float32 [768], replicated
- second_gain_gradient: float32 [768], replicated
- second_shift_gradient: float32 [768], replicated
- router_weight_gradient: float32 [768, 4], replicated
- expand_weight_gradient: float32 [4, 768, 3072], P('expert', None, 'tensor')
- expand_bias_gradient: float32 [4, 3072], P('expert', 'tensor')
- shrink_weight_gradient: float32 [4, 3072, 768], P('expert', 'tensor')
- shrink_bias_gradient: float32 [4, 768], P('expert')
The draws below stay inside these ranges and needn't reach their ends.
Inputs may be any that keep to these rules, and one draw needn't show every extreme that they name: `expert_choice`: each token names two different experts. One expert, the same for all groups, is the first choice of more than 392 tokens of every group. `slot_index`: within one group the routes to one expert are counted first choices before second choices, tokens in order; a kept route's slot is its count, so kept routes of one group to one expert have distinct slots; 391 is reached in every draw; a dropped route holds 391. `dropped`: 1 exactly for the routes beyond the first 392 of one group to one expert.
All inputs are finite; a program needn't handle non-finite values.
Results may differ from the reference program's by a relative error of at most 0.019.
Values may be sent and summed in bfloat16 or wider, within the bound.
No kernel may reach another device: no remote copies, remote signals or barrier semaphores. Data moves between devices by JAX's collectives and lax.ppermute only.
A program may use at most 192 MiB of HBM per device.

```python
import jax
import jax.numpy as jnp
from jax import lax

D = 768
H = 12
HD = 64
FF = 3072
SEQ = 197
IMG_DEV = 4
TOK_DEV = 788
GROUPS = 8
IMAGES = 32
EXPERTS = 4
CAP = 392


def route_table(key):
    base = jax.random.fold_in(key, 7)
    key_hot, key_score, key_other, key_step = jax.random.split(base, 4)
    hot_expert = jax.random.randint(key_hot, (), 0, EXPERTS, dtype=jnp.int32)
    scores = jax.random.randint(key_score, (GROUPS, TOK_DEV), 0, 2 ** 20, dtype=jnp.int32) * TOK_DEV + jnp.arange(TOK_DEV, dtype=jnp.int32)[None, :]
    placing = jnp.argsort(jnp.argsort(scores, axis=1), axis=1)
    hot_count = min(TOK_DEV, CAP + 8)
    other_expert = jax.random.randint(key_other, (GROUPS, TOK_DEV), 0, EXPERTS - 1, dtype=jnp.int32)
    other_expert = other_expert + (other_expert >= hot_expert).astype(jnp.int32)
    first_pick = jnp.where(placing < hot_count, hot_expert, other_expert).astype(jnp.int32)
    stride = jax.random.randint(key_step, (GROUPS, TOK_DEV), 1, EXPERTS, dtype=jnp.int32)
    second = (first_pick + stride) % EXPERTS
    ordered = jnp.concatenate([first_pick, second], axis=1)
    onehot = (ordered[:, :, None] == jnp.arange(EXPERTS, dtype=jnp.int32)[None, None, :]).astype(jnp.int32)
    before = jnp.cumsum(onehot, axis=1) - onehot
    position = jnp.sum(before * onehot, axis=2)
    slot_values = jnp.minimum(position, CAP - 1)
    dropped_values = (position >= CAP).astype(jnp.int32)

    def arrange(values):
        return jnp.stack([values[:, :TOK_DEV], values[:, TOK_DEV:]], axis=2).reshape(IMAGES, SEQ, 2).astype(jnp.int32)
    return (arrange(ordered), arrange(slot_values), arrange(dropped_values))


def draw_expert_choice(key, part):
    return route_table(key)[0]


def draw_slot_index(key, part):
    return route_table(key)[1]


def draw_dropped(key, part):
    return route_table(key)[2]


def level_of(own_key, shape, cuts, low, top_value):
    loudness = 1.0
    for dim, parts in cuts:
        steps = jax.random.uniform(jax.random.fold_in(jax.random.fold_in(own_key, 6), dim), (parts,), jnp.float32, low / len(cuts), top_value / len(cuts))
        loudness = loudness * jnp.repeat(jnp.exp(steps), shape[dim] // parts).reshape((-1,) + (1,) * (len(shape) - 1 - dim))
    return loudness


def gaussian(key, extent, width, reach, cuts=(), kind=jnp.bfloat16):
    loudness = level_of(key, extent, cuts, -0.22, 0.18) if cuts else 1.0
    entries = jax.random.normal(key, extent, jnp.float32) * width * loudness
    return jnp.minimum(jnp.maximum(entries, -reach), reach).astype(kind)


def setup_inputs(seed: int = 0) -> dict:
    key_list = jax.random.split(jax.random.key(seed), 19)
    return {
        "inputs": gaussian(key_list[0], (IMAGES, SEQ, D), 1.0, 6.0, ((0, 8),)),
        "first_gain": jnp.clip(1.0 + 0.1 * jax.random.normal(key_list[1], (D,), jnp.float32), 0.5, 1.5).astype(jnp.bfloat16),
        "first_shift": gaussian(key_list[2], (D,), 0.5, 3.0),
        "heads_weight": gaussian(key_list[3], (D, 3 * H * HD), D ** -0.5, 0.21875, ((1, 4),)),
        "heads_bias": gaussian(key_list[4], (H, 2 * HD), 0.5, 3.0, ((0, 4),)),
        "merge_weight": gaussian(key_list[5], (H * HD, D), (H * HD // 16) ** -0.5, 0.875, ((0, 4),)),
        "merge_bias": gaussian(key_list[6], (D,), 0.5, 3.0),
        "second_gain": jnp.clip(1.0 + 0.1 * jax.random.normal(key_list[7], (D,), jnp.float32), 0.5, 1.5).astype(jnp.bfloat16),
        "second_shift": gaussian(key_list[8], (D,), 0.5, 3.0),
        "router_weight": gaussian(key_list[9], (D, EXPERTS), (D // 2) ** -0.5, 0.3125),
        "expand_weight": gaussian(key_list[10], (EXPERTS, D, FF), D ** -0.5, 0.21875, ((0, 4), (2, 4))),
        "expand_bias": gaussian(key_list[11], (EXPERTS, FF), 0.5, 3.0, ((0, 4), (1, 4))),
        "shrink_weight": gaussian(key_list[12], (EXPERTS, FF, D), (max(1, FF // (EXPERTS * EXPERTS))) ** -0.5, 0.4375, ((0, 4), (1, 4))),
        "shrink_bias": gaussian(key_list[13], (EXPERTS, D), (1 + EXPERTS // 8), 4.0, ((0, 4),)),
        "cotangent": gaussian(key_list[14], (IMAGES, SEQ, D), 1.0, 6.0, ((0, 8),)),
        "expert_choice": draw_expert_choice(jax.random.fold_in(key_list[18], 71), 0),
        "slot_index": draw_slot_index(jax.random.fold_in(key_list[18], 71), 0),
        "dropped": draw_dropped(jax.random.fold_in(key_list[18], 71), 0),
    }


@jax.custom_vjp
def low(v):
    return lax.optimization_barrier(v.astype(jnp.bfloat16)).astype(jnp.float32)

@jax.custom_vjp
def low_back(v):
    return v

def low_keep(v):
    return (low(v), None)

def low_pass(kept, grad):
    return (grad,)

def back_keep(v):
    return (v, None)

def back_low(kept, grad):
    return (low(grad),)
low.defvjp(low_keep, low_pass)
low_back.defvjp(back_keep, back_low)
HIGHEST = lax.Precision.HIGHEST
EPSILON = 1e-06

def normalize(values, gain_vector, shift_vector):
    centre = values - lax.optimization_barrier(jnp.mean(values, axis=-1, keepdims=True))
    spread = lax.optimization_barrier(jnp.mean(centre * centre, axis=-1, keepdims=True))
    return centre * lax.rsqrt(spread + EPSILON) * gain_vector + shift_vector

def attention_block(normed, heads_weight, heads_bias, merge_weight):
    images = normed.shape[0]
    packed = jnp.einsum('bsd,dc->bsc', low(normed), heads_weight, precision=HIGHEST)
    packed = packed.reshape(images, SEQ, H, 3, HD)
    queries = low_back(low(packed[:, :, :, 0] + heads_bias[:, :HD]))
    key_rows = low_back(low(packed[:, :, :, 1]))
    values = low_back(low(packed[:, :, :, 2] + heads_bias[:, HD:]))
    scores = low_back(jnp.einsum('bqhd,bkhd->bhqk', queries, key_rows, precision=HIGHEST) * HD ** (-0.5))
    attention_probs = jax.nn.softmax(scores, axis=-1)
    context = jnp.einsum('bhqk,bkhd->bqhd', low(attention_probs), values, precision=HIGHEST)
    context = low_back(low(context.reshape(images, SEQ, H * HD)))
    return low_back(jnp.einsum('bsc,cd->bsd', context, merge_weight, precision=HIGHEST))

def expert_block(bundle):
    token_rows, expand_weight, expand_bias, shrink_weight, shrink_bias = bundle
    before_gelu = low_back(jnp.dot(token_rows, expand_weight, precision=HIGHEST) + expand_bias)
    hidden = low(jax.nn.gelu(before_gelu, approximate=False))
    return low_back(low(jnp.dot(hidden, shrink_weight, precision=HIGHEST) + shrink_bias))

def forward(inputs, first_gain, first_shift, heads_weight, heads_bias, merge_weight, merge_bias, second_gain, second_shift, router_weight, expand_weight, expand_bias, shrink_weight, shrink_bias, expert_choice, slot_index, dropped):
    blocks = inputs.reshape(GROUPS, IMG_DEV, SEQ, D)

    def attend(image_block):
        return attention_block(normalize(image_block, first_gain, first_shift), heads_weight, heads_bias, merge_weight)
    attended = lax.map(jax.checkpoint(attend), blocks)
    mixed_rows = (blocks + attended + merge_bias).reshape(GROUPS, TOK_DEV, D)
    normed = low(normalize(mixed_rows, second_gain, second_shift))
    logits = low_back(jnp.einsum('gtd,de->gte', normed, router_weight, precision=HIGHEST))
    router_probs = jax.nn.softmax(logits, axis=-1)
    kept_mask = (1 - dropped.reshape(GROUPS, TOK_DEV, 2)).astype(jnp.float32)
    picks = expert_choice.reshape(GROUPS, TOK_DEV, 2).astype(jnp.int32)
    route_gate = jnp.take_along_axis(router_probs, picks, axis=-1) * kept_mask
    target = picks * CAP + slot_index.reshape(GROUPS, TOK_DEV, 2).astype(jnp.int32)
    group_index = jnp.broadcast_to(jnp.arange(GROUPS, dtype=jnp.int32)[:, None, None], target.shape)
    dispatched = jnp.zeros((GROUPS, EXPERTS * CAP, D), jnp.float32)
    dispatched = dispatched.at[group_index, target].add(normed[:, :, None, :] * kept_mask[..., None])
    dispatched = low_back(dispatched)
    per_expert = dispatched.reshape(GROUPS, EXPERTS, CAP, D).transpose(1, 0, 2, 3).reshape(EXPERTS, GROUPS * CAP, D)
    answers = lax.map(jax.checkpoint(expert_block), (per_expert, expand_weight, expand_bias, shrink_weight, shrink_bias))
    answers = answers.reshape(EXPERTS, GROUPS, CAP, D).transpose(1, 0, 2, 3).reshape(GROUPS, EXPERTS * CAP, D)
    picked = answers[group_index, target]
    combined = mixed_rows + lax.optimization_barrier(jnp.sum(route_gate[..., None] * picked, axis=2))
    return combined.reshape(IMAGES, SEQ, D)

def reference(inputs, first_gain, first_shift, heads_weight, heads_bias, merge_weight, merge_bias, second_gain, second_shift, router_weight, expand_weight, expand_bias, shrink_weight, shrink_bias, cotangent, expert_choice, slot_index, dropped):
    floats = [member.astype(jnp.float32) for member in (inputs, first_gain, first_shift, heads_weight, heads_bias, merge_weight, merge_bias, second_gain, second_shift, router_weight, expand_weight, expand_bias, shrink_weight, shrink_bias)]

    def closed(*params):
        return forward(*params, expert_choice, slot_index, dropped)
    result, pullback = jax.vjp(closed, *floats)
    gradients = pullback(cotangent.astype(jnp.float32))
    return (result.astype(jnp.bfloat16), gradients[0], gradients[1], gradients[2], gradients[3], gradients[4], gradients[5], gradients[6], gradients[7], gradients[8], gradients[9], gradients[10], gradients[11], gradients[12], gradients[13])
```

```python
import jax
import jax.numpy as jnp
from jax import lax
from jax.sharding import PartitionSpec as P

EPSILON = 1e-06
BF = jnp.bfloat16
F32 = jnp.float32


def up_to(value, step):
    return (value + step - 1) // step * step


def dot(a, b, contract, out=F32):
    return lax.dot_general(a, b, ((contract[:1], contract[1:]), ((), ())), preferred_element_type=F32).astype(out)


def core_swap(v):
    n = lax.axis_size("tensor")
    return lax.ppermute(v, "tensor", [(i, i ^ 1) for i in range(n)])


def side_swap(v):
    n = lax.axis_size("tensor")
    return lax.ppermute(v, "tensor", [(i, i ^ 2) for i in range(n)])


def half_swap(v):
    n = lax.axis_size("dp")
    return lax.ppermute(v, "dp", [(i, i ^ 1) for i in range(n)])


def shift_expert(v, step):
    n = lax.axis_size("expert")
    return lax.ppermute(v, "expert", [(i, (i + step) % n) for i in range(n)])


def roll_blocks(v, start):
    size = v.shape[0]
    return lax.dynamic_slice_in_dim(jnp.concatenate([v, v], axis=0), start % size, size, 0)


def to_owners(blocks):
    n = lax.axis_size("expert")
    if n <= 8:
        return [blocks[0]] + [shift_expert(blocks[j], j) for j in range(1, n)]
    z = lax.axis_index("expert")
    canon = roll_blocks(blocks, n - z)
    got = lax.all_to_all(canon, "expert", split_axis=0, concat_axis=0, tiled=True)
    return [got[j] for j in range(n)]


def from_owners(blocks):
    n = lax.axis_size("expert")
    if n <= 8:
        return [blocks[0]] + [shift_expert(blocks[j], n - j) for j in range(1, n)]
    z = lax.axis_index("expert")
    got = lax.all_to_all(blocks, "expert", split_axis=0, concat_axis=0, tiled=True)
    got = roll_blocks(got, z)
    return [got[j] for j in range(n)]


def in_order(first, mine, other, axis):
    return jnp.where(
        first, jnp.concatenate([mine, other], axis=axis), jnp.concatenate([other, mine], axis=axis)
    )


def sum_dense(part):
    d = lax.axis_index("dp")
    z = lax.axis_index("expert")
    n = lax.axis_size("expert")
    size, columns = part.shape
    cut = part.reshape(2, n, size // (2 * n), columns)
    keep = jnp.where(d == 0, cut[0], cut[1])
    send = jnp.where(d == 0, cut[1], cut[0]).astype(BF)
    summed = keep + half_swap(send).astype(F32)
    low = summed.astype(BF)
    if n <= 8:
        own = lax.dynamic_index_in_dim(summed, z, 0, keepdims=False)
        for j in range(1, n):
            block = lax.dynamic_index_in_dim(low, (z + j) % n, 0, keepdims=False)
            own = own + shift_expert(block, j).astype(F32)
        own = own.astype(BF)
        gathered = [shift_expert(own, j) for j in range(n - 1, 0, -1)] + [own]
        gathered = roll_blocks(jnp.stack(gathered), n - 1 - z)
    else:
        got = lax.all_to_all(low, "expert", split_axis=0, concat_axis=0, tiled=True)
        own = jnp.sum(got.astype(F32), axis=0).astype(BF)
        gathered = lax.all_gather(own, "expert", axis=0)
    other = half_swap(gathered)
    return in_order(d == 0, gathered[None], other[None], 0).astype(F32).reshape(size, columns)


def stats(v):
    centre = v - jnp.mean(v, axis=-1, keepdims=True)
    scale = lax.rsqrt(jnp.mean(centre * centre, axis=-1, keepdims=True) + EPSILON)
    return centre * scale, scale


def norm_back(grad, unit, scale, gain):
    g = grad * gain
    return scale * (
        g - jnp.mean(g, axis=-1, keepdims=True) - unit * jnp.mean(g * unit, axis=-1, keepdims=True)
    )


def per_device(
    inputs,
    first_gain,
    first_shift,
    heads_weight,
    heads_bias,
    merge_weight,
    merge_bias,
    second_gain,
    second_shift,
    router_weight,
    expand_weight,
    expand_bias,
    shrink_weight,
    shrink_bias,
    cotangent,
    expert_choice,
    slot_index,
    dropped,
):
    images, length, width = inputs.shape
    seq = up_to(length, 8)
    rows = images * seq
    half = rows // 2
    wide = width // 2
    head_count = heads_bias.shape[0]
    head_size = heads_bias.shape[1] // 2
    score_scale = head_size ** (-0.5)
    experts = router_weight.shape[1]
    real_rows = images * length
    capacity = max(8, min(real_rows // 2 // 8 * 8, (3 * real_rows // experts + 7) // 8 * 8))
    part_slots = up_to((capacity + 1) // 2, 8)
    t = lax.axis_index("tensor")
    c, y = t % 2, t // 2
    z = lax.axis_index("expert")
    c0, y0 = c == 0, y == 0

    def rows_of(v, which):
        return lax.dynamic_slice_in_dim(v, which * half, half, 0)

    def pad_rows(v):
        return jnp.pad(v, ((0, 0), (0, seq - length), (0, 0))).reshape(rows, v.shape[2])

    expand_own, shrink_own = expand_weight[0], shrink_weight[0]
    expand_both = jnp.concatenate([expand_own, core_swap(expand_own)], axis=1)
    shrink_both = jnp.concatenate([shrink_own, core_swap(shrink_own)], axis=0)
    hidden_here = expand_own.shape[1]
    bias_both = jnp.concatenate([expand_bias, core_swap(expand_bias)], axis=1).astype(F32)
    shrink_keep = jnp.where(y0, shrink_both[:, :wide], shrink_both[:, wide:])
    shrink_send = jnp.where(y0, shrink_both[:, wide:], shrink_both[:, :wide])
    expand_keep = jnp.where(y0, expand_both[:wide], expand_both[wide:])
    expand_send = jnp.where(y0, expand_both[wide:], expand_both[:wide])
    shrink_bias_half = jnp.where(y0, shrink_bias[:, :wide], shrink_bias[:, wide:]).astype(F32)
    merge_pair = in_order(y0, merge_weight[None], side_swap(merge_weight)[None], 0)
    merge_full = in_order(c0, merge_pair[:, None], core_swap(merge_pair)[:, None], 1).reshape(-1, width)
    router_rel = lax.dynamic_slice_in_dim(
        jnp.concatenate([router_weight, router_weight], axis=1), z, experts, 1
    )

    kept = jnp.pad(1 - dropped, ((0, 0), (0, seq - length), (0, 0))).reshape(rows, 2) > 0
    relative = (pad_rows(expert_choice) - z + experts) % experts
    slots = pad_rows(slot_index)
    slot_half = slots // part_slots
    slot_row = slots - slot_half * part_slots
    send_key = jnp.where(kept & (slot_half == c), relative * part_slots + slot_row, -1).T
    slot_iota = lax.broadcasted_iota(jnp.int32, (experts * part_slots, rows), 0)
    pick = ((slot_iota == send_key[0][None, :]) | (slot_iota == send_key[1][None, :])).astype(BF)
    back_key = jnp.where(kept, relative * part_slots + slot_row, -1)
    back_own = rows_of(jnp.where(slot_half == c, back_key, -1), c)
    back_other = rows_of(jnp.where(slot_half == c, -1, back_key), c)
    back_iota = lax.broadcasted_iota(jnp.int32, (half, experts * part_slots), 1)
    place_own = ((back_iota == back_own[:, :1]) | (back_iota == back_own[:, 1:])).astype(BF)
    place_other = ((back_iota == back_other[:, :1]) | (back_iota == back_other[:, 1:])).astype(BF)

    cot = pad_rows(cotangent)
    cot_out = dot(pick, cot, (1, 0), BF).reshape(experts, part_slots, width)
    cot_rows = jnp.concatenate(to_owners(cot_out), axis=0)

    residual = pad_rows(inputs).astype(F32)
    gain_one, shift_one = first_gain.astype(F32), first_shift.astype(F32)
    first_low = (stats(residual)[0] * gain_one + shift_one).astype(BF)
    packed = dot(first_low, heads_weight, (1, 0)).reshape(images, seq, head_count, 3, head_size)
    bias_float = heads_bias.astype(F32)
    queries = (packed[:, :, :, 0] + bias_float[:, :head_size]).astype(BF)
    key_rows = packed[:, :, :, 1].astype(BF)
    values = (packed[:, :, :, 2] + bias_float[:, head_size:]).astype(BF)
    scores = (
        jnp.einsum("bqhd,bkhd->bhqk", queries, key_rows, preferred_element_type=F32) * score_scale
    )
    key_real = lax.broadcasted_iota(jnp.int32, (1, 1, 1, seq), 3) < length
    scores = jnp.where(key_real, scores, -1e30)
    powers = jnp.exp(scores - jnp.max(scores, axis=-1, keepdims=True))
    attention_probs = powers / jnp.sum(powers, axis=-1, keepdims=True)
    probs_low = attention_probs.astype(BF)
    context = jnp.einsum("bhqk,bkhd->bqhd", probs_low, values, preferred_element_type=F32)
    context = context.reshape(rows, head_count * head_size).astype(BF)

    context_pair = in_order(c0, rows_of(context, c), core_swap(rows_of(context, 1 - c)), 1)
    context_all = in_order(y0, context_pair, side_swap(context_pair), 1)
    residual_half = rows_of(residual, c)
    mixed = residual_half + dot(context_all, merge_full, (1, 0)) + merge_bias.astype(F32)
    unit_two, scale_two = stats(mixed)
    gain_two = second_gain.astype(F32)
    second_low = (unit_two * gain_two + second_shift.astype(F32)).astype(BF)
    second_all = in_order(c0, second_low, core_swap(second_low), 0)
    router_probs = jax.nn.softmax(dot(second_low, router_rel, (1, 0)), axis=-1)

    sent = dot(pick, second_all, (1, 0), BF).reshape(experts, part_slots, width)
    received = jnp.concatenate(to_owners(sent), axis=0)
    before = dot(received, expand_both, (1, 0)) + bias_both
    share = 0.5 * (1.0 + lax.erf(before * (0.5**0.5)))
    hidden = (before * share).astype(BF)
    slope = share + before * jnp.exp(-0.5 * before * before) * (0.5 / jnp.pi) ** 0.5
    answers = (
        dot(hidden, shrink_keep, (1, 0))
        + side_swap(dot(hidden, shrink_send, (1, 0), BF)).astype(F32)
        + shrink_bias_half
    ).astype(BF)

    slot_gate = jax.nn.softmax(dot(received, router_rel, (1, 0)), axis=-1)[:, :1]
    answer_grad = (slot_gate * cot_rows.astype(F32)).astype(BF)
    slot_bias_part = jnp.sum(answer_grad, axis=0, dtype=F32)
    before_grad = (dot(answer_grad, shrink_both, (1, 1)) * slope).astype(BF)
    expand_bias_part = jnp.sum(before_grad, axis=0, dtype=F32)
    dispatch_grad = (
        dot(before_grad, expand_keep, (1, 1))
        + side_swap(dot(before_grad, expand_send, (1, 1), BF)).astype(F32)
    ).astype(BF)
    shrink_part = dot(hidden, answer_grad, (0, 0))
    expand_part = dot(received, before_grad, (0, 0))

    shrink_low = (
        shrink_part[:hidden_here] + core_swap(shrink_part[hidden_here:].astype(BF)).astype(F32)
    ).astype(BF)
    expand_low = (
        expand_part[:, :hidden_here] + core_swap(expand_part[:, hidden_here:].astype(BF)).astype(F32)
    ).astype(BF)
    shrink_sum = shrink_low.astype(F32) + half_swap(shrink_low).astype(F32)
    expand_sum = expand_low.astype(F32) + half_swap(expand_low).astype(F32)
    bias_pair = jnp.stack([slot_bias_part, expand_bias_part[:hidden_here]]) + core_swap(
        jnp.stack([slot_bias_part, expand_bias_part[hidden_here:]])
    )
    bias_pair = bias_pair + half_swap(bias_pair)

    back = jnp.stack(from_owners(answers.reshape(experts, part_slots, wide)))
    back_pair = core_swap(back)
    picked = [
        dot(place_own[:, j * part_slots : (j + 1) * part_slots], back[j], (1, 0))
        + dot(place_other[:, j * part_slots : (j + 1) * part_slots], back_pair[j], (1, 0))
        for j in range(experts)
    ]
    cot_half = rows_of(cot, c).astype(F32)
    cot_side = jnp.where(y0, cot_half[:, :wide], cot_half[:, wide:])
    combined = jnp.where(y0, mixed[:, :wide], mixed[:, wide:]) + sum(
        router_probs[:, j : j + 1] * picked[j] for j in range(experts)
    )
    out_side = combined.astype(BF)
    out_rows = in_order(y0, out_side, side_swap(out_side), 1)
    outputs = in_order(c0, out_rows, core_swap(out_rows), 0).reshape(images, seq, width)[:, :length]
    prob_part = jnp.stack([jnp.sum(cot_side * picked[j], axis=1) for j in range(experts)])
    prob_grad = (prob_part + side_swap(prob_part)).T
    logit_grad = (
        router_probs * (prob_grad - jnp.sum(router_probs * prob_grad, axis=1, keepdims=True))
    ).astype(BF)
    router_part = dot(logit_grad, second_low, (0, 0))
    router_part = roll_blocks(router_part, experts - z)
    from_router = dot(logit_grad, router_rel, (1, 1))

    grads = jnp.stack(from_owners(dispatch_grad.reshape(experts, part_slots, wide)))
    grads_pair = core_swap(grads)
    grad_side = (
        dot(place_own, grads.reshape(-1, wide), (1, 0))
        + dot(place_other, grads_pair.reshape(-1, wide), (1, 0))
    ).astype(BF)
    grad_rows = in_order(y0, grad_side, side_swap(grad_side), 1)
    normed_grad = from_router + grad_rows.astype(F32)
    mixed_grad = cot_half + norm_back(normed_grad, unit_two, scale_two, gain_two)
    attended_half = mixed_grad.astype(BF)
    attended_grad = in_order(c0, attended_half, core_swap(attended_half), 0)
    second_gain_part = jnp.sum(normed_grad * unit_two, axis=0)
    second_shift_part = jnp.sum(normed_grad, axis=0)
    merge_bias_part = jnp.sum(mixed_grad, axis=0)

    merge_sum = sum_dense(dot(context, attended_grad, (0, 0)))
    context_grad = dot(attended_grad, merge_weight, (1, 1), BF)
    context_grad = context_grad.reshape(images, seq, head_count, head_size)
    weight_grad = jnp.einsum("bqhd,bkhd->bhqk", context_grad, values, preferred_element_type=F32)
    value_grad = jnp.einsum(
        "bhqk,bqhd->bkhd", probs_low, context_grad, preferred_element_type=F32
    ).astype(BF)
    balance = jnp.sum(attention_probs * weight_grad, axis=-1, keepdims=True)
    score_grad = (attention_probs * (weight_grad - balance)).astype(BF)
    query_grad = (
        jnp.einsum("bhqk,bkhd->bqhd", score_grad, key_rows, preferred_element_type=F32) * score_scale
    ).astype(BF)
    key_grad = (
        jnp.einsum("bhqk,bqhd->bkhd", score_grad, queries, preferred_element_type=F32) * score_scale
    ).astype(BF)
    heads_bias_part = jnp.concatenate(
        [
            jnp.sum(query_grad, axis=(0, 1), dtype=F32),
            jnp.sum(value_grad, axis=(0, 1), dtype=F32),
        ],
        axis=1,
    )
    packed_grad = jnp.stack([query_grad, key_grad, value_grad], axis=3).reshape(
        rows, head_count * 3 * head_size
    )
    heads_sum = sum_dense(dot(first_low, packed_grad, (0, 0)))

    first_send = dot(rows_of(packed_grad, 1 - c), heads_weight, (1, 1), BF)
    first_low_sum = (
        dot(rows_of(packed_grad, c), heads_weight, (1, 1)) + core_swap(first_send).astype(F32)
    ).astype(BF)
    first_grad = first_low_sum.astype(F32) + side_swap(first_low_sum).astype(F32)
    unit_one, scale_one = stats(residual_half)
    input_half = mixed_grad + norm_back(first_grad, unit_one, scale_one, gain_one)
    input_gradient = in_order(c0, input_half, core_swap(input_half), 0).reshape(images, seq, width)[
        :, :length
    ]

    first_gain_part = jnp.sum(first_grad * unit_one, axis=0)
    first_shift_part = jnp.sum(first_grad, axis=0)
    small = jnp.concatenate(
        [
            jnp.stack(
                [
                    first_gain_part,
                    first_shift_part,
                    merge_bias_part,
                    second_gain_part,
                    second_shift_part,
                ]
            ),
            router_part,
        ],
        axis=0,
    )
    small = small + core_swap(small)
    head_row = jnp.pad(heads_bias_part.reshape(1, -1), ((0, 0), (0, width - heads_bias_part.size)))
    small = jnp.concatenate([small, head_row], axis=0)
    n = lax.axis_size("expert")
    step = 1
    while step < n:
        small = small + lax.ppermute(small, "expert", [(i, i ^ step) for i in range(n)])
        step *= 2
    small = small + half_swap(small)
    heads_bias_sum = small[5 + experts, : heads_bias_part.size].reshape(heads_bias_part.shape)
    return (
        outputs,
        input_gradient,
        small[0],
        small[1],
        heads_sum,
        heads_bias_sum,
        merge_sum,
        small[2],
        small[3],
        small[4],
        small[5 : 5 + experts].T,
        expand_sum[None],
        bias_pair[1][None],
        shrink_sum[None],
        bias_pair[0][None],
    )


def solution(mesh):
    placed = (
        P(("dp", "expert"), None, None),
        P(),
        P(),
        P(None, "tensor"),
        P("tensor", None),
        P("tensor", None),
        P(),
        P(),
        P(),
        P(),
        P("expert", None, "tensor"),
        P("expert", "tensor"),
        P("expert", "tensor", None),
        P("expert", None),
        P(("dp", "expert"), None, None),
        P(("dp", "expert"), None, None),
        P(("dp", "expert"), None, None),
        P(("dp", "expert"), None, None),
    )
    return jax.shard_map(
        per_device,
        mesh=mesh,
        in_specs=placed,
        out_specs=(
            P(("dp", "expert"), None, None),
            P(("dp", "expert"), None, None),
            P(),
            P(),
            P(None, "tensor"),
            P("tensor", None),
            P("tensor", None),
            P(),
            P(),
            P(),
            P(),
            P("expert", None, "tensor"),
            P("expert", "tensor"),
            P("expert", "tensor", None),
            P("expert", None),
        ),
        check_vma=False,
    )
```

```python
import jax
import jax.numpy as jnp
from jax import lax
from jax.sharding import PartitionSpec as P


EPSILON = 1e-06
BF = jnp.bfloat16
F32 = jnp.float32


def up_to(value, step):
    return (value + step - 1) // step * step


def dot(a, b, contract, out=F32):
    return lax.dot_general(a, b, ((contract[:1], contract[1:]), ((), ())), preferred_element_type=F32).astype(out)


def swap(v, axis, bit):
    n = lax.axis_size(axis)
    return lax.ppermute(v, axis, [(i, i ^ bit) for i in range(n)])


def core_swap(v):
    return swap(v, "tensor", 1)


def side_swap(v):
    return swap(v, "tensor", 2)


def half_swap(v):
    return swap(v, "dp", 1)


def shift_expert(v, step):
    n = lax.axis_size("expert")
    return lax.ppermute(v, "expert", [(i, (i + step) % n) for i in range(n)])


def roll_blocks(v, start):
    size = v.shape[0]
    return lax.dynamic_slice_in_dim(jnp.concatenate([v, v], axis=0), start % size, size, 0)


def to_owners(blocks):
    n = lax.axis_size("expert")
    if n <= 8:
        return [blocks[0]] + [shift_expert(blocks[j], j) for j in range(1, n)]
    z = lax.axis_index("expert")
    canon = roll_blocks(blocks, n - z)
    got = lax.all_to_all(canon, "expert", split_axis=0, concat_axis=0, tiled=True)
    return [got[j] for j in range(n)]


def from_owners(blocks):
    n = lax.axis_size("expert")
    if n <= 8:
        return [blocks[0]] + [shift_expert(blocks[j], n - j) for j in range(1, n)]
    z = lax.axis_index("expert")
    got = lax.all_to_all(blocks, "expert", split_axis=0, concat_axis=0, tiled=True)
    got = roll_blocks(got, z)
    return [got[j] for j in range(n)]


def in_order(first, mine, other, axis):
    return jnp.where(
        first, jnp.concatenate([mine, other], axis=axis), jnp.concatenate([other, mine], axis=axis)
    )


def sum_dense(part):
    d = lax.axis_index("dp")
    z = lax.axis_index("expert")
    n = lax.axis_size("expert")
    size, columns = part.shape
    cut = part.reshape(2, n, size // (2 * n), columns)
    keep = jnp.where(d == 0, cut[0], cut[1])
    send = jnp.where(d == 0, cut[1], cut[0]).astype(BF)
    summed = keep + half_swap(send).astype(F32)
    low = summed.astype(BF)
    if n <= 8:
        own = lax.dynamic_index_in_dim(summed, z, 0, keepdims=False)
        for j in range(1, n):
            block = lax.dynamic_index_in_dim(low, (z + j) % n, 0, keepdims=False)
            own = own + shift_expert(block, j).astype(F32)
        own = own.astype(BF)
        gathered = [shift_expert(own, j) for j in range(n - 1, 0, -1)] + [own]
        gathered = roll_blocks(jnp.stack(gathered), n - 1 - z)
    else:
        got = lax.all_to_all(low, "expert", split_axis=0, concat_axis=0, tiled=True)
        own = jnp.sum(got.astype(F32), axis=0).astype(BF)
        gathered = lax.all_gather(own, "expert", axis=0)
    other = half_swap(gathered)
    return in_order(d == 0, gathered[None], other[None], 0).astype(F32).reshape(size, columns)


def stats(v):
    centre = v - jnp.mean(v, axis=-1, keepdims=True)
    scale = lax.rsqrt(jnp.mean(centre * centre, axis=-1, keepdims=True) + EPSILON)
    return centre * scale, scale


def norm_back(grad, unit, scale, gain):
    g = grad * gain
    return scale * (
        g - jnp.mean(g, axis=-1, keepdims=True) - unit * jnp.mean(g * unit, axis=-1, keepdims=True)
    )


def whole_block(
    inputs,
    first_gain,
    first_shift,
    heads_weight,
    heads_bias,
    merge_weight,
    merge_bias,
    second_gain,
    second_shift,
    router_weight,
    expand_weight,
    expand_bias,
    shrink_weight,
    shrink_bias,
    cotangent,
    expert_choice,
    slot_index,
    dropped,
):
    images, length, width = inputs.shape
    seq = up_to(length, 8)
    rows = images * seq
    half = rows // 2
    wide = width // 2
    head_count = heads_bias.shape[0]
    head_size = heads_bias.shape[1] // 2
    score_scale = head_size ** (-0.5)
    experts = router_weight.shape[1]
    real_rows = images * length
    capacity = max(8, min(real_rows // 2 // 8 * 8, (3 * real_rows // experts + 7) // 8 * 8))
    part_slots = up_to((capacity + 1) // 2, 8)
    t = lax.axis_index("tensor")
    c, y = t % 2, t // 2
    z = lax.axis_index("expert")
    c0, y0 = c == 0, y == 0

    def rows_of(v, which):
        return lax.dynamic_slice_in_dim(v, which * half, half, 0)

    def pad_rows(v):
        return jnp.pad(v, ((0, 0), (0, seq - length), (0, 0))).reshape(rows, v.shape[2])

    def half_rows(v):
        v = lax.dynamic_slice_in_dim(v, c * (images // 2), images // 2, 0)
        return jnp.pad(v, ((0, 0), (0, seq - length), (0, 0))).reshape(half, width).astype(F32)

    def both_halves(mine, other):
        mine = mine.reshape(images // 2, seq, width)[:, :length]
        other = other.reshape(images // 2, seq, width)[:, :length]
        return in_order(c0, mine, other, 0)

    expand_own, shrink_own = expand_weight[0], shrink_weight[0]
    expand_both = jnp.concatenate([expand_own, core_swap(expand_own)], axis=1)
    shrink_both = jnp.concatenate([shrink_own, core_swap(shrink_own)], axis=0)
    hidden_here = expand_own.shape[1]
    bias_both = jnp.concatenate([expand_bias, core_swap(expand_bias)], axis=1).astype(F32)
    shrink_keep = jnp.where(y0, shrink_both[:, :wide], shrink_both[:, wide:])
    shrink_send = jnp.where(y0, shrink_both[:, wide:], shrink_both[:, :wide])
    expand_keep = jnp.where(y0, expand_both[:wide], expand_both[wide:])
    expand_send = jnp.where(y0, expand_both[wide:], expand_both[:wide])
    shrink_bias_half = jnp.where(y0, shrink_bias[:, :wide], shrink_bias[:, wide:]).astype(F32)
    merge_pair = in_order(y0, merge_weight[None], side_swap(merge_weight)[None], 0)
    merge_full = in_order(c0, merge_pair[:, None], core_swap(merge_pair)[:, None], 1).reshape(-1, width)
    router_rel = lax.dynamic_slice_in_dim(
        jnp.concatenate([router_weight, router_weight], axis=1), z, experts, 1
    )

    kept = jnp.pad(1 - dropped, ((0, 0), (0, seq - length), (0, 0))).reshape(rows, 2) > 0
    relative = (pad_rows(expert_choice) - z + experts) % experts
    slots = pad_rows(slot_index)
    slot_half = slots // part_slots
    slot_row = slots - slot_half * part_slots
    send_key = jnp.where(kept & (slot_half == c), relative * part_slots + slot_row, -1).T
    slot_iota = lax.broadcasted_iota(jnp.int32, (experts * part_slots, rows), 0)
    pick = ((slot_iota == send_key[0][None, :]) | (slot_iota == send_key[1][None, :])).astype(BF)
    back_key = jnp.where(kept, relative * part_slots + slot_row, -1)
    back_own = rows_of(jnp.where(slot_half == c, back_key, -1), c)
    back_other = rows_of(jnp.where(slot_half == c, -1, back_key), c)
    back_iota = lax.broadcasted_iota(jnp.int32, (half, experts * part_slots), 1)
    place_own = ((back_iota == back_own[:, :1]) | (back_iota == back_own[:, 1:])).astype(BF)
    place_other = ((back_iota == back_other[:, :1]) | (back_iota == back_other[:, 1:])).astype(BF)

    cot = pad_rows(cotangent)
    cot_out = dot(pick, cot, (1, 0), BF).reshape(experts, part_slots, width)
    cot_rows = jnp.concatenate(to_owners(cot_out), axis=0)

    residual = pad_rows(inputs).astype(F32)
    gain_one, shift_one = first_gain.astype(F32), first_shift.astype(F32)
    first_low = (stats(residual)[0] * gain_one + shift_one).astype(BF)
    packed = dot(first_low, heads_weight, (1, 0)).reshape(images, seq, head_count, 3, head_size)
    bias_float = heads_bias.astype(F32)
    queries = (packed[:, :, :, 0] + bias_float[:, :head_size]).astype(BF)
    key_rows = packed[:, :, :, 1].astype(BF)
    values = (packed[:, :, :, 2] + bias_float[:, head_size:]).astype(BF)
    scores = (
        jnp.einsum("bqhd,bkhd->bhqk", queries, key_rows, preferred_element_type=F32) * score_scale
    )
    key_real = lax.broadcasted_iota(jnp.int32, (1, 1, 1, seq), 3) < length
    scores = jnp.where(key_real, scores, -1e30)
    powers = jnp.exp(scores - jnp.max(scores, axis=-1, keepdims=True))
    attention_probs = powers / jnp.sum(powers, axis=-1, keepdims=True)
    probs_low = attention_probs.astype(BF)
    context = jnp.einsum("bhqk,bkhd->bqhd", probs_low, values, preferred_element_type=F32)
    context = context.reshape(rows, head_count * head_size).astype(BF)

    context_pair = in_order(c0, rows_of(context, c), core_swap(rows_of(context, 1 - c)), 1)
    context_all = in_order(y0, context_pair, side_swap(context_pair), 1)
    residual_half = half_rows(inputs)
    mixed = residual_half + dot(context_all, merge_full, (1, 0)) + merge_bias.astype(F32)
    unit_two, scale_two = stats(mixed)
    gain_two = second_gain.astype(F32)
    second_low = (unit_two * gain_two + second_shift.astype(F32)).astype(BF)
    second_all = in_order(c0, second_low, core_swap(second_low), 0)
    router_probs = jax.nn.softmax(dot(second_low, router_rel, (1, 0)), axis=-1)

    sent = dot(pick, second_all, (1, 0), BF).reshape(experts, part_slots, width)
    received = jnp.concatenate(to_owners(sent), axis=0)
    before = dot(received, expand_both, (1, 0)) + bias_both
    share = 0.5 * (1.0 + lax.erf(before * (0.5**0.5)))
    hidden = (before * share).astype(BF)
    slope = share + before * jnp.exp(-0.5 * before * before) * (0.5 / jnp.pi) ** 0.5
    answers = (
        dot(hidden, shrink_keep, (1, 0))
        + side_swap(dot(hidden, shrink_send, (1, 0), BF)).astype(F32)
        + shrink_bias_half
    ).astype(BF)

    slot_gate = jax.nn.softmax(dot(received, router_rel, (1, 0)), axis=-1)[:, :1]
    answer_grad = lax.optimization_barrier((slot_gate * cot_rows.astype(F32)).astype(BF))
    slot_bias_part = jnp.sum(answer_grad, axis=0, dtype=F32)
    before_grad = (dot(answer_grad, shrink_both, (1, 1)) * slope).astype(BF)
    expand_bias_part = jnp.sum(before_grad, axis=0, dtype=F32)
    dispatch_grad = (
        dot(before_grad, expand_keep, (1, 1))
        + side_swap(dot(before_grad, expand_send, (1, 1), BF)).astype(F32)
    ).astype(BF)
    shrink_part = dot(hidden, answer_grad, (0, 0))
    expand_part = dot(received, before_grad, (0, 0))

    shrink_low = (
        shrink_part[:hidden_here] + core_swap(shrink_part[hidden_here:].astype(BF)).astype(F32)
    ).astype(BF)
    expand_low = (
        expand_part[:, :hidden_here] + core_swap(expand_part[:, hidden_here:].astype(BF)).astype(F32)
    ).astype(BF)
    shrink_sum = shrink_low.astype(F32) + half_swap(shrink_low).astype(F32)
    expand_sum = expand_low.astype(F32) + half_swap(expand_low).astype(F32)

    back = jnp.stack(from_owners(answers.reshape(experts, part_slots, wide)))
    back_pair = core_swap(back)
    picked = [
        dot(place_own[:, j * part_slots : (j + 1) * part_slots], back[j], (1, 0))
        + dot(place_other[:, j * part_slots : (j + 1) * part_slots], back_pair[j], (1, 0))
        for j in range(experts)
    ]
    cot_half = half_rows(cotangent)
    cot_side = jnp.where(y0, cot_half[:, :wide], cot_half[:, wide:])
    combined = jnp.where(y0, mixed[:, :wide], mixed[:, wide:]) + sum(
        router_probs[:, j : j + 1] * picked[j] for j in range(experts)
    )
    out_side = combined.astype(BF)
    out_rows = in_order(y0, out_side, side_swap(out_side), 1)
    outputs = both_halves(out_rows, core_swap(out_rows))
    prob_part = jnp.stack([jnp.sum(cot_side * picked[j], axis=1) for j in range(experts)])
    prob_grad = (prob_part + side_swap(prob_part)).T
    logit_grad = (
        router_probs * (prob_grad - jnp.sum(router_probs * prob_grad, axis=1, keepdims=True))
    ).astype(BF)
    router_part = dot(logit_grad, second_low, (0, 0))
    router_part = roll_blocks(router_part, experts - z)
    from_router = dot(logit_grad, router_rel, (1, 1))

    grads = jnp.stack(from_owners(dispatch_grad.reshape(experts, part_slots, wide)))
    grads_pair = core_swap(grads)
    grad_side = (
        dot(place_own, grads.reshape(-1, wide), (1, 0))
        + dot(place_other, grads_pair.reshape(-1, wide), (1, 0))
    ).astype(BF)
    grad_rows = in_order(y0, grad_side, side_swap(grad_side), 1)
    normed_grad = from_router + grad_rows.astype(F32)
    mixed_grad = cot_half + norm_back(normed_grad, unit_two, scale_two, gain_two)
    attended_half = mixed_grad.astype(BF)
    attended_grad = in_order(c0, attended_half, core_swap(attended_half), 0)
    second_gain_part = jnp.sum(normed_grad * unit_two, axis=0)
    second_shift_part = jnp.sum(normed_grad, axis=0)
    merge_bias_part = jnp.sum(mixed_grad, axis=0)

    merge_sum = sum_dense(dot(context, attended_grad, (0, 0)))
    context_grad = dot(attended_grad, merge_weight, (1, 1), BF)
    context_grad = context_grad.reshape(images, seq, head_count, head_size)
    weight_grad = jnp.einsum("bqhd,bkhd->bhqk", context_grad, values, preferred_element_type=F32)
    value_grad = jnp.einsum(
        "bhqk,bqhd->bkhd", probs_low, context_grad, preferred_element_type=F32
    ).astype(BF)
    balance = jnp.sum(attention_probs * weight_grad, axis=-1, keepdims=True)
    score_grad = (attention_probs * (weight_grad - balance)).astype(BF)
    query_grad = (
        jnp.einsum("bhqk,bkhd->bqhd", score_grad, key_rows, preferred_element_type=F32) * score_scale
    ).astype(BF)
    key_grad = (
        jnp.einsum("bhqk,bqhd->bkhd", score_grad, queries, preferred_element_type=F32) * score_scale
    ).astype(BF)
    heads_bias_part = jnp.concatenate(
        [
            jnp.sum(query_grad, axis=(0, 1), dtype=F32),
            jnp.sum(value_grad, axis=(0, 1), dtype=F32),
        ],
        axis=1,
    )
    packed_grad = jnp.stack([query_grad, key_grad, value_grad], axis=3).reshape(
        rows, head_count * 3 * head_size
    )
    heads_part = dot(first_low, packed_grad, (0, 0))
    heads_sum = sum_dense(heads_part)

    first_send = dot(rows_of(packed_grad, 1 - c), heads_weight, (1, 1), BF)
    first_low_sum = (
        dot(rows_of(packed_grad, c), heads_weight, (1, 1)) + core_swap(first_send).astype(F32)
    ).astype(BF)
    first_grad = first_low_sum.astype(F32) + side_swap(first_low_sum).astype(F32)
    unit_one, scale_one = stats(residual_half)
    input_half = mixed_grad + norm_back(first_grad, unit_one, scale_one, gain_one)
    input_gradient = both_halves(input_half, core_swap(input_half))

    first_gain_part = jnp.sum(first_grad * unit_one, axis=0)
    first_shift_part = jnp.sum(first_grad, axis=0)
    small = jnp.concatenate(
        [
            jnp.stack(
                [
                    first_gain_part,
                    first_shift_part,
                    merge_bias_part,
                    second_gain_part,
                    second_shift_part,
                ]
            ),
            router_part,
        ],
        axis=0,
    )
    count = small.shape[0]
    pair = jnp.stack([slot_bias_part, expand_bias_part[:hidden_here]])
    pair_send = jnp.stack([slot_bias_part, expand_bias_part[hidden_here:]])
    got = core_swap(jnp.concatenate([small, pair_send], axis=0))
    small, pair = small + got[:count], pair + got[count:]
    head_row = jnp.pad(heads_bias_part.reshape(1, -1), ((0, 0), (0, width - heads_bias_part.size)))
    small = jnp.concatenate([small, head_row], axis=0)
    n = lax.axis_size("expert")
    step = 1
    while step < n:
        small = small + lax.ppermute(small, "expert", [(i, i ^ step) for i in range(n)])
        step *= 2
    last = jnp.concatenate([small, pair], axis=0)
    last = last + half_swap(last)
    small, pair = last[: count + 1], last[count + 1 :]
    heads_bias_sum = small[5 + experts, : heads_bias_part.size].reshape(heads_bias_part.shape)
    return (
        outputs,
        input_gradient,
        small[0],
        small[1],
        heads_sum,
        heads_bias_sum,
        merge_sum,
        small[2],
        small[3],
        small[4],
        small[5 : 5 + experts].T,
        expand_sum[None],
        pair[1][None],
        shrink_sum[None],
        pair[0][None],
    )


def solution(mesh):
    placed = (
        P(("dp", "expert"), None, None),
        P(),
        P(),
        P(None, "tensor"),
        P("tensor", None),
        P("tensor", None),
        P(),
        P(),
        P(),
        P(),
        P("expert", None, "tensor"),
        P("expert", "tensor"),
        P("expert", "tensor", None),
        P("expert", None),
        P(("dp", "expert"), None, None),
        P(("dp", "expert"), None, None),
        P(("dp", "expert"), None, None),
        P(("dp", "expert"), None, None),
    )
    return jax.shard_map(
        whole_block,
        mesh=mesh,
        in_specs=placed,
        out_specs=(
            P(("dp", "expert"), None, None),
            P(("dp", "expert"), None, None),
            P(),
            P(),
            P(None, "tensor"),
            P("tensor", None),
            P("tensor", None),
            P(),
            P(),
            P(),
            P(),
            P("expert", None, "tensor"),
            P("expert", "tensor"),
            P("expert", "tensor", None),
            P("expert", None),
        ),
        check_vma=False,
    )
```

```python
import jax
import jax.numpy as jnp
from jax import lax
from jax.sharding import PartitionSpec as P


EPSILON = 1e-06
DP, EXPERT, TENSOR = "dp", "expert", "tensor"
BF = jnp.bfloat16
F32 = jnp.float32


def up_to(value, step):
    return (value + step - 1) // step * step


def dot(a, b, contract, out=F32):
    return lax.dot_general(a, b, ((contract[:1], contract[1:]), ((), ())), preferred_element_type=F32).astype(out)


def swap(v, axis, bit):
    n = lax.axis_size(axis)
    return lax.ppermute(v, axis, [(i, i ^ bit) for i in range(n)])


def core_swap(v):
    return swap(v, TENSOR, 1)


def side_swap(v):
    return swap(v, TENSOR, 2)


def half_swap(v):
    return swap(v, DP, 1)


def shift_expert(v, step):
    n = lax.axis_size(EXPERT)
    return lax.ppermute(v, EXPERT, [(i, (i + step) % n) for i in range(n)])


def roll_blocks(v, start):
    size = v.shape[0]
    return lax.dynamic_slice_in_dim(jnp.concatenate([v, v], axis=0), start % size, size, 0)


def to_owners(blocks):
    n = lax.axis_size(EXPERT)
    if n <= 8:
        return [blocks[0]] + [shift_expert(blocks[j], j) for j in range(1, n)]
    z = lax.axis_index(EXPERT)
    canon = roll_blocks(blocks, n - z)
    got = lax.all_to_all(canon, EXPERT, split_axis=0, concat_axis=0, tiled=True)
    return [got[j] for j in range(n)]


def from_owners(blocks):
    n = lax.axis_size(EXPERT)
    if n <= 8:
        return [blocks[0]] + [shift_expert(blocks[j], n - j) for j in range(1, n)]
    z = lax.axis_index(EXPERT)
    got = lax.all_to_all(blocks, EXPERT, split_axis=0, concat_axis=0, tiled=True)
    got = roll_blocks(got, z)
    return [got[j] for j in range(n)]


def in_order(first, mine, other, axis):
    return jnp.where(
        first, jnp.concatenate([mine, other], axis=axis), jnp.concatenate([other, mine], axis=axis)
    )


def sum_dense(part):
    d = lax.axis_index(DP)
    z = lax.axis_index(EXPERT)
    n = lax.axis_size(EXPERT)
    size, columns = part.shape
    cut = part.reshape(2, n, size // (2 * n), columns)
    keep = jnp.where(d == 0, cut[0], cut[1])
    send = jnp.where(d == 0, cut[1], cut[0]).astype(BF)
    summed = keep + half_swap(send).astype(F32)
    low = summed.astype(BF)
    if n <= 8:
        own = lax.dynamic_index_in_dim(summed, z, 0, keepdims=False)
        for j in range(1, n):
            block = lax.dynamic_index_in_dim(low, (z + j) % n, 0, keepdims=False)
            own = own + shift_expert(block, j).astype(F32)
        own = own.astype(BF)
        gathered = [shift_expert(own, j) for j in range(n - 1, 0, -1)] + [own]
        gathered = roll_blocks(jnp.stack(gathered), n - 1 - z)
    else:
        got = lax.all_to_all(low, EXPERT, split_axis=0, concat_axis=0, tiled=True)
        own = jnp.sum(got.astype(F32), axis=0).astype(BF)
        gathered = lax.all_gather(own, EXPERT, axis=0)
    other = half_swap(gathered)
    return in_order(d == 0, gathered[None], other[None], 0).astype(F32).reshape(size, columns)


def stats(v):
    centre = v - jnp.mean(v, axis=-1, keepdims=True)
    scale = lax.rsqrt(jnp.mean(centre * centre, axis=-1, keepdims=True) + EPSILON)
    return centre * scale, scale


def norm_back(grad, unit, scale, gain):
    g = grad * gain
    return scale * (
        g - jnp.mean(g, axis=-1, keepdims=True) - unit * jnp.mean(g * unit, axis=-1, keepdims=True)
    )


def whole_block(
    inputs,
    first_gain,
    first_shift,
    heads_weight,
    heads_bias,
    merge_weight,
    merge_bias,
    second_gain,
    second_shift,
    router_weight,
    expand_weight,
    expand_bias,
    shrink_weight,
    shrink_bias,
    cotangent,
    expert_choice,
    slot_index,
    dropped,
):
    images, length, width = inputs.shape
    seq = up_to(length, 8)
    rows = images * seq
    half = rows // 2
    wide = width // 2
    head_count = heads_bias.shape[0]
    head_size = heads_bias.shape[1] // 2
    score_scale = head_size ** (-0.5)
    experts = router_weight.shape[1]
    real_rows = images * length
    capacity = max(8, min(real_rows // 2 // 8 * 8, (3 * real_rows // experts + 7) // 8 * 8))
    part_slots = up_to((capacity + 1) // 2, 8)
    t = lax.axis_index(TENSOR)
    c, y = t % 2, t // 2
    z = lax.axis_index(EXPERT)
    c0, y0 = c == 0, y == 0

    def rows_of(v, which):
        return lax.dynamic_slice_in_dim(v, which * half, half, 0)

    def pad_rows(v):
        return jnp.pad(v, ((0, 0), (0, seq - length), (0, 0))).reshape(rows, v.shape[2])

    def half_rows(v):
        v = lax.dynamic_slice_in_dim(v, c * (images // 2), images // 2, 0)
        return jnp.pad(v, ((0, 0), (0, seq - length), (0, 0))).reshape(half, width).astype(F32)

    def both_halves(mine, other):
        mine = mine.reshape(images // 2, seq, width)[:, :length]
        other = other.reshape(images // 2, seq, width)[:, :length]
        return in_order(c0, mine, other, 0)

    kept = jnp.pad(1 - dropped, ((0, 0), (0, seq - length), (0, 0))).reshape(rows, 2) > 0
    relative = (pad_rows(expert_choice) - z + experts) % experts
    slots = pad_rows(slot_index)
    slot_half = slots // part_slots
    slot_row = slots - slot_half * part_slots
    send_key = jnp.where(kept & (slot_half == c), relative * part_slots + slot_row, -1).T
    slot_iota = lax.broadcasted_iota(jnp.int32, (experts * part_slots, rows), 0)
    pick = ((slot_iota == send_key[0][None, :]) | (slot_iota == send_key[1][None, :])).astype(BF)
    cot_out = dot(pick, pad_rows(cotangent), (1, 0), BF).reshape(experts, part_slots, width)
    cot_rows = jnp.concatenate(to_owners(cot_out), axis=0)

    expand_own, shrink_own = expand_weight[0], shrink_weight[0]
    expand_both = jnp.concatenate([expand_own, core_swap(expand_own)], axis=1)
    shrink_both = jnp.concatenate([shrink_own, core_swap(shrink_own)], axis=0)
    hidden_here = expand_own.shape[1]
    bias_both = jnp.concatenate([expand_bias, core_swap(expand_bias)], axis=1).astype(F32)
    shrink_keep = jnp.where(y0, shrink_both[:, :wide], shrink_both[:, wide:])
    shrink_send = jnp.where(y0, shrink_both[:, wide:], shrink_both[:, :wide])
    expand_keep = jnp.where(y0, expand_both[:wide], expand_both[wide:])
    expand_send = jnp.where(y0, expand_both[wide:], expand_both[:wide])
    shrink_bias_half = jnp.where(y0, shrink_bias[:, :wide], shrink_bias[:, wide:]).astype(F32)
    merge_pair = in_order(y0, merge_weight[None], side_swap(merge_weight)[None], 0)
    merge_full = in_order(c0, merge_pair[:, None], core_swap(merge_pair)[:, None], 1).reshape(-1, width)
    router_rel = lax.dynamic_slice_in_dim(
        jnp.concatenate([router_weight, router_weight], axis=1), z, experts, 1
    )

    residual = pad_rows(inputs).astype(F32)
    gain_one, shift_one = first_gain.astype(F32), first_shift.astype(F32)
    first_low = (stats(residual)[0] * gain_one + shift_one).astype(BF)
    packed = dot(first_low, heads_weight, (1, 0))
    packed = packed.reshape(images, seq, head_count, 3, head_size)
    bias_float = heads_bias.astype(F32)
    queries = (packed[:, :, :, 0] + bias_float[:, :head_size]).astype(BF)
    key_rows = packed[:, :, :, 1].astype(BF)
    values = (packed[:, :, :, 2] + bias_float[:, head_size:]).astype(BF)
    scores = (
        jnp.einsum("bqhd,bkhd->bhqk", queries, key_rows, preferred_element_type=F32) * score_scale
    )
    key_real = lax.broadcasted_iota(jnp.int32, (1, 1, 1, seq), 3) < length
    scores = jnp.where(key_real, scores, -1e30)
    powers = jnp.exp(scores - jnp.max(scores, axis=-1, keepdims=True))
    attention_probs = powers / jnp.sum(powers, axis=-1, keepdims=True)
    probs_low = attention_probs.astype(BF)
    context = jnp.einsum("bhqk,bkhd->bqhd", probs_low, values, preferred_element_type=F32)
    context = context.reshape(rows, head_count * head_size).astype(BF)

    context_pair = in_order(c0, rows_of(context, c), core_swap(rows_of(context, 1 - c)), 1)
    context_all = in_order(y0, context_pair, side_swap(context_pair), 1)
    mixed = half_rows(inputs) + dot(context_all, merge_full, (1, 0)) + merge_bias.astype(F32)
    unit_two, scale_two = stats(mixed)
    gain_two = second_gain.astype(F32)
    second_low = (unit_two * gain_two + second_shift.astype(F32)).astype(BF)
    second_all = in_order(c0, second_low, core_swap(second_low), 0)
    router_probs = jax.nn.softmax(dot(second_low, router_rel, (1, 0)), axis=-1)

    sent = dot(pick, second_all, (1, 0), BF).reshape(experts, part_slots, width)
    received = jnp.concatenate(to_owners(sent), axis=0)
    back_key = jnp.where(kept, relative * part_slots + slot_row, -1)
    back_own = rows_of(jnp.where(slot_half == c, back_key, -1), c)
    back_other = rows_of(jnp.where(slot_half == c, -1, back_key), c)
    back_iota = lax.broadcasted_iota(jnp.int32, (half, experts * part_slots), 1)
    place_own = ((back_iota == back_own[:, :1]) | (back_iota == back_own[:, 1:])).astype(BF)
    place_other = ((back_iota == back_other[:, :1]) | (back_iota == back_other[:, 1:])).astype(BF)
    cot_half = half_rows(cotangent)
    unit_one, scale_one = stats(half_rows(inputs))
    before = dot(received, expand_both, (1, 0)) + bias_both
    share = 0.5 * (1.0 + lax.erf(before * (0.5**0.5)))
    hidden = (before * share).astype(BF)
    slope = share + before * jnp.exp(-0.5 * before * before) * (0.5 / jnp.pi) ** 0.5
    answers = (
        dot(hidden, shrink_keep, (1, 0))
        + side_swap(dot(hidden, shrink_send, (1, 0), BF)).astype(F32)
        + shrink_bias_half
    ).astype(BF)

    slot_gate = jax.nn.softmax(dot(received, router_rel, (1, 0)), axis=-1)[:, :1]
    answer_grad = lax.optimization_barrier((slot_gate * cot_rows.astype(F32)).astype(BF))
    slot_bias_part = jnp.sum(answer_grad, axis=0, dtype=F32)
    before_grad = (dot(answer_grad, shrink_both, (1, 1)) * slope).astype(BF)
    expand_bias_part = jnp.sum(before_grad, axis=0, dtype=F32)
    dispatch_grad = (
        dot(before_grad, expand_keep, (1, 1))
        + side_swap(dot(before_grad, expand_send, (1, 1), BF)).astype(F32)
    ).astype(BF)
    shrink_part = dot(hidden, answer_grad, (0, 0))
    expand_part = dot(received, before_grad, (0, 0))

    shrink_pair = core_swap(shrink_part[hidden_here:].astype(BF)).astype(F32)
    shrink_low = (shrink_part[:hidden_here] + shrink_pair).astype(BF)
    expand_pair = core_swap(expand_part[:, hidden_here:].astype(BF)).astype(F32)
    expand_low = (expand_part[:, :hidden_here] + expand_pair).astype(BF)
    shrink_got = half_swap(shrink_low)
    expand_got = half_swap(expand_low)

    back = jnp.stack(from_owners(answers.reshape(experts, part_slots, wide)))
    back_pair = core_swap(back)
    picked = [
        dot(place_own[:, j * part_slots : (j + 1) * part_slots], back[j], (1, 0))
        + dot(place_other[:, j * part_slots : (j + 1) * part_slots], back_pair[j], (1, 0))
        for j in range(experts)
    ]
    cot_side = jnp.where(y0, cot_half[:, :wide], cot_half[:, wide:])
    combined = jnp.where(y0, mixed[:, :wide], mixed[:, wide:]) + sum(
        router_probs[:, j : j + 1] * picked[j] for j in range(experts)
    )
    out_side = combined.astype(BF)
    out_rows = in_order(y0, out_side, side_swap(out_side), 1)
    out_pair = core_swap(out_rows)
    outputs = both_halves(out_rows, out_pair)
    prob_part = jnp.stack([jnp.sum(cot_side * picked[j], axis=1) for j in range(experts)])
    prob_grad = (prob_part + side_swap(prob_part)).T
    logit_grad = (
        router_probs * (prob_grad - jnp.sum(router_probs * prob_grad, axis=1, keepdims=True))
    ).astype(BF)
    router_part = dot(logit_grad, second_low, (0, 0))
    router_part = roll_blocks(router_part, experts - z)
    from_router = dot(logit_grad, router_rel, (1, 1))

    grads = jnp.stack(from_owners(dispatch_grad.reshape(experts, part_slots, wide)))
    grads_pair = core_swap(grads)
    grad_side = (
        dot(place_own, grads.reshape(-1, wide), (1, 0))
        + dot(place_other, grads_pair.reshape(-1, wide), (1, 0))
    ).astype(BF)
    grad_rows = in_order(y0, grad_side, side_swap(grad_side), 1)
    normed_grad = from_router + grad_rows.astype(F32)
    mixed_grad = cot_half + norm_back(normed_grad, unit_two, scale_two, gain_two)
    attended_half = mixed_grad.astype(BF)
    attended_grad = in_order(c0, attended_half, core_swap(attended_half), 0)
    second_gain_part = jnp.sum(normed_grad * unit_two, axis=0)
    second_shift_part = jnp.sum(normed_grad, axis=0)
    merge_bias_part = jnp.sum(mixed_grad, axis=0)

    context_grad = dot(attended_grad, merge_weight, (1, 1), BF)
    context_grad = context_grad.reshape(images, seq, head_count, head_size)
    weight_grad = jnp.einsum("bqhd,bkhd->bhqk", context_grad, values, preferred_element_type=F32)
    value_grad = jnp.einsum(
        "bhqk,bqhd->bkhd", probs_low, context_grad, preferred_element_type=F32
    ).astype(BF)
    balance = jnp.sum(attention_probs * weight_grad, axis=-1, keepdims=True)
    score_grad = (attention_probs * (weight_grad - balance)).astype(BF)
    query_grad = (
        jnp.einsum("bhqk,bkhd->bqhd", score_grad, key_rows, preferred_element_type=F32) * score_scale
    ).astype(BF)
    key_grad = (
        jnp.einsum("bhqk,bqhd->bkhd", score_grad, queries, preferred_element_type=F32) * score_scale
    ).astype(BF)
    heads_bias_part = jnp.concatenate(
        [
            jnp.sum(query_grad, axis=(0, 1), dtype=F32),
            jnp.sum(value_grad, axis=(0, 1), dtype=F32),
        ],
        axis=1,
    )
    packed_grad = jnp.stack([query_grad, key_grad, value_grad], axis=3).reshape(
        rows, head_count * 3 * head_size
    )
    shrink_sum = (shrink_low.astype(F32) + shrink_got.astype(F32))[None]
    expand_sum = (expand_low.astype(F32) + expand_got.astype(F32))[None]
    heads_part = dot(packed_grad, first_low, (0, 0))
    merge_part = dot(context, attended_grad, (0, 0))
    dense_sum = sum_dense(jnp.concatenate([heads_part, merge_part], axis=0))
    heads_sum = dense_sum[: packed_grad.shape[1]].T
    merge_sum = dense_sum[packed_grad.shape[1] :]

    first_send = dot(rows_of(packed_grad, 1 - c), heads_weight, (1, 1), BF)
    first_got = core_swap(first_send).astype(F32)
    first_low_sum = (dot(rows_of(packed_grad, c), heads_weight, (1, 1)) + first_got).astype(BF)
    first_grad = first_low_sum.astype(F32) + side_swap(first_low_sum).astype(F32)
    first_gain_part = jnp.sum(first_grad * unit_one, axis=0)
    first_shift_part = jnp.sum(first_grad, axis=0)
    input_half = mixed_grad + norm_back(first_grad, unit_one, scale_one, gain_one)
    input_pair = core_swap(input_half)
    input_gradient = both_halves(input_half, input_pair)

    count = 5 + experts
    lines = up_to(count + 3, 8)
    line = lax.broadcasted_iota(jnp.int32, (lines, 1), 0)
    head_row = jnp.pad(heads_bias_part.reshape(-1), (0, width - heads_bias_part.size))
    vectors = (
        first_gain_part,
        first_shift_part,
        merge_bias_part,
        second_gain_part,
        second_shift_part,
    )
    shared = jnp.pad(router_part, ((5, lines - count), (0, 0)))
    for k, vector in enumerate(vectors):
        shared = shared + jnp.where(line == k, vector[None, :], 0.0)
    shared = shared + jnp.where(line == count, slot_bias_part[None, :], 0.0)
    sent_small = shared + jnp.where(line == count + 1, expand_bias_part[None, hidden_here:], 0.0)
    small = shared + jnp.where(line == count + 1, expand_bias_part[None, :hidden_here], 0.0)
    small = small + jnp.where(line == count + 2, head_row[None, :], 0.0)
    small = small + core_swap(sent_small)
    over_experts = (line < count) | (line == count + 2)
    n = lax.axis_size(EXPERT)
    step = 1
    while step < n:
        got = lax.ppermute(small, EXPERT, [(i, i ^ step) for i in range(n)])
        small = small + jnp.where(over_experts, got, 0.0)
        step *= 2
    small = small + half_swap(small)
    heads_bias_sum = small[count + 2, : heads_bias_part.size].reshape(heads_bias_part.shape)
    return (
        outputs,
        input_gradient,
        small[0],
        small[1],
        heads_sum,
        heads_bias_sum,
        merge_sum,
        small[2],
        small[3],
        small[4],
        small[5:count].T,
        expand_sum,
        small[None, count + 1],
        shrink_sum,
        small[None, count],
    )


def solution(mesh):
    placed = (
        P((DP, EXPERT), None, None),
        P(),
        P(),
        P(None, TENSOR),
        P(TENSOR, None),
        P(TENSOR, None),
        P(),
        P(),
        P(),
        P(),
        P(EXPERT, None, TENSOR),
        P(EXPERT, TENSOR),
        P(EXPERT, TENSOR, None),
        P(EXPERT, None),
        P((DP, EXPERT), None, None),
        P((DP, EXPERT), None, None),
        P((DP, EXPERT), None, None),
        P((DP, EXPERT), None, None),
    )
    return jax.shard_map(
        whole_block,
        mesh=mesh,
        in_specs=placed,
        out_specs=(
            P((DP, EXPERT), None, None),
            P((DP, EXPERT), None, None),
            P(),
            P(),
            P(None, TENSOR),
            P(TENSOR, None),
            P(TENSOR, None),
            P(),
            P(),
            P(),
            P(),
            P(EXPERT, None, TENSOR),
            P(EXPERT, TENSOR),
            P(EXPERT, TENSOR, None),
            P(EXPERT, None),
        ),
        check_vma=False,
    )
```

```python
import jax
import jax.numpy as jnp
import numpy as np
from jax import lax
from jax.sharding import PartitionSpec as P


EPSILON = 1e-06
DP, EXPERT, TENSOR = "dp", "expert", "tensor"
BF = jnp.bfloat16
F32 = jnp.float32


def up_to(value, step):
    return (value + step - 1) // step * step


def dot(a, b, contract, out=F32):
    return lax.dot_general(a, b, ((contract[:1], contract[1:]), ((), ())), preferred_element_type=F32).astype(out)


def swap(v, axis, bit):
    n = lax.axis_size(axis)
    return lax.ppermute(v, axis, [(i, i ^ bit) for i in range(n)])


def core_swap(v):
    return swap(v, TENSOR, 1)


def side_swap(v):
    return swap(v, TENSOR, 2)


def half_swap(v):
    return swap(v, DP, 1)


def shift_expert(v, step):
    n = lax.axis_size(EXPERT)
    return lax.ppermute(v, EXPERT, [(i, (i + step) % n) for i in range(n)])


def roll_blocks(v, start):
    size = v.shape[0]
    return lax.dynamic_slice_in_dim(jnp.concatenate([v, v], axis=0), start % size, size, 0)


def to_owners(blocks):
    n = lax.axis_size(EXPERT)
    if n <= 8:
        return [blocks[0]] + [shift_expert(blocks[j], j) for j in range(1, n)]
    z = lax.axis_index(EXPERT)
    canon = roll_blocks(blocks, n - z)
    got = lax.all_to_all(canon, EXPERT, split_axis=0, concat_axis=0, tiled=True)
    return [got[j] for j in range(n)]


def from_owners(blocks):
    n = lax.axis_size(EXPERT)
    if n <= 8:
        return [blocks[0]] + [shift_expert(blocks[j], n - j) for j in range(1, n)]
    z = lax.axis_index(EXPERT)
    got = lax.all_to_all(blocks, EXPERT, split_axis=0, concat_axis=0, tiled=True)
    got = roll_blocks(got, z)
    return [got[j] for j in range(n)]


def in_order(first, mine, other, axis):
    return jnp.where(
        first, jnp.concatenate([mine, other], axis=axis), jnp.concatenate([other, mine], axis=axis)
    )


def sum_dense(part):
    d = lax.axis_index(DP)
    z = lax.axis_index(EXPERT)
    n = lax.axis_size(EXPERT)
    size, columns = part.shape
    cut = part.reshape(2, n, size // (2 * n), columns)
    keep = jnp.where(d == 0, cut[0], cut[1])
    send = jnp.where(d == 0, cut[1], cut[0]).astype(BF)

    summed = keep + half_swap(send).astype(F32)
    low = summed.astype(BF)
    if n <= 8:
        own = lax.dynamic_index_in_dim(summed, z, 0, keepdims=False)
        for j in range(1, n):
            block = lax.dynamic_index_in_dim(low, (z + j) % n, 0, keepdims=False)
            own = own + shift_expert(block, j).astype(F32)
        own = own.astype(BF)
        own_other = half_swap(own)
        pieces = jnp.stack([shift_expert(own, j) for j in range(n - 1, 0, -1)])
        others = half_swap(pieces)
        gathered = roll_blocks(jnp.concatenate([pieces, own[None]], axis=0), n - 1 - z)
        other = roll_blocks(jnp.concatenate([others, own_other[None]], axis=0), n - 1 - z)
    else:
        got = lax.all_to_all(low, EXPERT, split_axis=0, concat_axis=0, tiled=True)
        own = jnp.sum(got.astype(F32), axis=0).astype(BF)
        gathered = lax.all_gather(own, EXPERT, axis=0)
        other = half_swap(gathered)
    return in_order(d == 0, gathered[None], other[None], 0).astype(F32).reshape(size, columns)


def stats(v):
    centre = v - jnp.mean(v, axis=-1, keepdims=True)
    scale = lax.rsqrt(jnp.mean(centre * centre, axis=-1, keepdims=True) + EPSILON)
    return centre * scale, scale


def norm_back(grad, unit, scale, gain):
    g = grad * gain
    return scale * (
        g - jnp.mean(g, axis=-1, keepdims=True) - unit * jnp.mean(g * unit, axis=-1, keepdims=True)
    )


def whole_block(
    inputs,
    first_gain,
    first_shift,
    heads_weight,
    heads_bias,
    merge_weight,
    merge_bias,
    second_gain,
    second_shift,
    router_weight,
    expand_weight,
    expand_bias,
    shrink_weight,
    shrink_bias,
    cotangent,
    expert_choice,
    slot_index,
    dropped,
):
    images, length, width = inputs.shape
    seq = up_to(length, 8)
    rows = images * seq
    half = rows // 2
    wide = width // 2
    head_count = heads_bias.shape[0]
    head_size = heads_bias.shape[1] // 2
    score_scale = head_size ** (-0.5)
    experts = router_weight.shape[1]
    real_rows = images * length
    capacity = max(8, min(real_rows // 2 // 8 * 8, (3 * real_rows // experts + 7) // 8 * 8))
    part_slots = up_to((capacity + 1) // 2, 8)
    t = lax.axis_index(TENSOR)
    c, y = t % 2, t // 2
    z = lax.axis_index(EXPERT)
    c0, y0 = c == 0, y == 0

    def rows_of(v, which):
        return lax.dynamic_slice_in_dim(v, which * half, half, 0)

    def pad_rows(v):
        return jnp.pad(v, ((0, 0), (0, seq - length), (0, 0))).reshape(rows, v.shape[2])

    def half_rows(v):
        v = lax.dynamic_slice_in_dim(v, c * (images // 2), images // 2, 0)
        return jnp.pad(v, ((0, 0), (0, seq - length), (0, 0))).reshape(half, width).astype(F32)

    def both_halves(mine, other):
        mine = mine.reshape(images // 2, seq, width)[:, :length]
        other = other.reshape(images // 2, seq, width)[:, :length]
        return in_order(c0, mine, other, 0)

    kept = jnp.pad(1 - dropped, ((0, 0), (0, seq - length), (0, 0))).reshape(rows, 2) > 0
    relative = (pad_rows(expert_choice) - z + experts) % experts
    slots = pad_rows(slot_index)
    slot_half = slots // part_slots
    slot_row = slots - slot_half * part_slots
    send_key = jnp.where(kept & (slot_half == c), relative * part_slots + slot_row, -1).T
    slot_iota = lax.broadcasted_iota(jnp.int32, (experts * part_slots, rows), 0)
    pick = ((slot_iota == send_key[0][None, :]) | (slot_iota == send_key[1][None, :])).astype(BF)
    cot_out = dot(pick, pad_rows(cotangent), (1, 0), BF).reshape(experts, part_slots, width)
    cot_rows = jnp.concatenate(to_owners(cot_out), axis=0)

    expand_own, shrink_own = expand_weight[0], shrink_weight[0]
    expand_both = jnp.concatenate([expand_own, core_swap(expand_own)], axis=1)
    shrink_both = jnp.concatenate([shrink_own, core_swap(shrink_own)], axis=0)
    hidden_here = expand_own.shape[1]
    bias_pair = core_swap(expand_bias)
    bias_both = jnp.concatenate([expand_bias, bias_pair], axis=1).astype(F32)
    shrink_keep = jnp.where(y0, shrink_both[:, :wide], shrink_both[:, wide:])
    shrink_send = jnp.where(y0, shrink_both[:, wide:], shrink_both[:, :wide])
    expand_keep = jnp.where(y0, expand_both[:wide], expand_both[wide:])
    expand_send = jnp.where(y0, expand_both[wide:], expand_both[:wide])
    shrink_bias_half = jnp.where(y0, shrink_bias[:, :wide], shrink_bias[:, wide:]).astype(F32)
    merge_pair = in_order(y0, merge_weight[None], side_swap(merge_weight)[None], 0)
    merge_full = in_order(c0, merge_pair[:, None], core_swap(merge_pair)[:, None], 1).reshape(-1, width)
    router_rel = lax.dynamic_slice_in_dim(
        jnp.concatenate([router_weight, router_weight], axis=1), z, experts, 1
    )

    residual = pad_rows(inputs).astype(F32)
    gain_one, shift_one = first_gain.astype(F32), first_shift.astype(F32)
    first_low = (stats(residual)[0] * gain_one + shift_one).astype(BF)
    packed = dot(first_low, heads_weight, (1, 0))
    packed = packed.reshape(images, seq, head_count, 3, head_size)
    bias_float = heads_bias.astype(F32)
    queries = (packed[:, :, :, 0] + bias_float[:, :head_size]).astype(BF)
    key_rows = packed[:, :, :, 1].astype(BF)
    values = (packed[:, :, :, 2] + bias_float[:, head_size:]).astype(BF)
    scores = (
        jnp.einsum("bqhd,bkhd->bhqk", queries, key_rows, preferred_element_type=F32) * score_scale
    )
    key_real = lax.broadcasted_iota(jnp.int32, (1, 1, 1, seq), 3) < length
    scores = jnp.where(key_real, scores, -1e30)
    powers = jnp.exp(scores - jnp.max(scores, axis=-1, keepdims=True))
    attention_probs = powers / jnp.sum(powers, axis=-1, keepdims=True)
    probs_low = attention_probs.astype(BF)
    context = jnp.einsum("bhqk,bkhd->bqhd", probs_low, values, preferred_element_type=F32)
    context = context.reshape(rows, head_count * head_size).astype(BF)

    context_pair = in_order(c0, rows_of(context, c), core_swap(rows_of(context, 1 - c)), 1)
    context_all = in_order(y0, context_pair, side_swap(context_pair), 1)
    mixed = half_rows(inputs) + dot(context_all, merge_full, (1, 0)) + merge_bias.astype(F32)
    unit_two, scale_two = stats(mixed)
    gain_two = second_gain.astype(F32)
    second_low = (unit_two * gain_two + second_shift.astype(F32)).astype(BF)
    second_all = in_order(c0, second_low, core_swap(second_low), 0)
    router_probs = jax.nn.softmax(dot(second_low, router_rel, (1, 0)), axis=-1)

    sent = dot(pick, second_all, (1, 0), BF).reshape(experts, part_slots, width)
    received = jnp.concatenate(to_owners(sent), axis=0)
    back_key = jnp.where(kept, relative * part_slots + slot_row, -1)
    back_own = rows_of(jnp.where(slot_half == c, back_key, -1), c)
    back_other = rows_of(jnp.where(slot_half == c, -1, back_key), c)
    back_iota = lax.broadcasted_iota(jnp.int32, (half, experts * part_slots), 1)
    place_own = ((back_iota == back_own[:, :1]) | (back_iota == back_own[:, 1:])).astype(BF)
    place_other = ((back_iota == back_other[:, :1]) | (back_iota == back_other[:, 1:])).astype(BF)
    cot_half = half_rows(cotangent)
    unit_one, scale_one = stats(half_rows(inputs))
    before = dot(received, expand_both, (1, 0)) + bias_both
    share = 0.5 * (1.0 + lax.erf(before * (0.5**0.5)))
    hidden = (before * share).astype(BF)
    slope = share + before * jnp.exp(-0.5 * before * before) * (0.5 / jnp.pi) ** 0.5
    answers = (
        dot(hidden, shrink_keep, (1, 0))
        + side_swap(dot(hidden, shrink_send, (1, 0), BF)).astype(F32)
        + shrink_bias_half
    ).astype(BF)

    slot_gate = jax.nn.softmax(dot(received, router_rel, (1, 0)), axis=-1)[:, :1]
    answer_grad = lax.optimization_barrier((slot_gate * cot_rows.astype(F32)).astype(BF))
    slot_bias_part = jnp.sum(answer_grad, axis=0, dtype=F32)
    before_grad = (dot(answer_grad, shrink_both, (1, 1)) * slope).astype(BF)
    expand_bias_part = jnp.sum(before_grad, axis=0, dtype=F32)
    dispatch_grad = (
        dot(before_grad, expand_keep, (1, 1))
        + side_swap(dot(before_grad, expand_send, (1, 1), BF)).astype(F32)
    ).astype(BF)
    shrink_part = dot(hidden, answer_grad, (0, 0))
    expand_part = dot(received, before_grad, (0, 0))

    shrink_pair = core_swap(shrink_part[hidden_here:].astype(BF)).astype(F32)
    shrink_low = (shrink_part[:hidden_here] + shrink_pair).astype(BF)
    expand_pair = core_swap(expand_part[:, hidden_here:].astype(BF)).astype(F32)
    expand_low = (expand_part[:, :hidden_here] + expand_pair).astype(BF)
    shrink_got = half_swap(shrink_low)
    expand_got = half_swap(expand_low)

    back = from_owners(answers.reshape(experts, part_slots, wide))
    back = jnp.stack(back)
    back_pair = core_swap(back)
    picked = [
        dot(place_own[:, j * part_slots : (j + 1) * part_slots], back[j], (1, 0))
        + dot(place_other[:, j * part_slots : (j + 1) * part_slots], back_pair[j], (1, 0))
        for j in range(experts)
    ]
    cot_side = jnp.where(y0, cot_half[:, :wide], cot_half[:, wide:])
    combined = jnp.where(y0, mixed[:, :wide], mixed[:, wide:]) + sum(
        router_probs[:, j : j + 1] * picked[j] for j in range(experts)
    )
    out_side = combined.astype(BF)
    out_got = side_swap(out_side)
    out_rows = in_order(y0, out_side, out_got, 1)
    out_pair = core_swap(out_rows)
    outputs = both_halves(out_rows, out_pair)
    prob_part = jnp.stack([jnp.sum(cot_side * picked[j], axis=1) for j in range(experts)])
    prob_got = side_swap(prob_part)
    prob_grad = (prob_part + prob_got).T
    logit_grad = (
        router_probs * (prob_grad - jnp.sum(router_probs * prob_grad, axis=1, keepdims=True))
    ).astype(BF)
    router_part = dot(logit_grad, second_low, (0, 0))
    router_part = roll_blocks(router_part, experts - z)
    from_router = dot(logit_grad, router_rel, (1, 1))

    grads = jnp.stack(from_owners(dispatch_grad.reshape(experts, part_slots, wide)))
    grads_pair = core_swap(grads)
    grad_side = (
        dot(place_own, grads.reshape(-1, wide), (1, 0))
        + dot(place_other, grads_pair.reshape(-1, wide), (1, 0))
    ).astype(BF)
    grad_rows = in_order(y0, grad_side, side_swap(grad_side), 1)
    normed_grad = from_router + grad_rows.astype(F32)
    mixed_grad = cot_half + norm_back(normed_grad, unit_two, scale_two, gain_two)
    attended_half = mixed_grad.astype(BF)
    attended_grad = in_order(c0, attended_half, core_swap(attended_half), 0)
    second_gain_part = jnp.sum(normed_grad * unit_two, axis=0)
    second_shift_part = jnp.sum(normed_grad, axis=0)
    merge_bias_part = jnp.sum(mixed_grad, axis=0)

    context_grad = dot(attended_grad, merge_weight, (1, 1), BF)
    context_grad = context_grad.reshape(images, seq, head_count, head_size)
    weight_grad = jnp.einsum("bqhd,bkhd->bhqk", context_grad, values, preferred_element_type=F32)
    value_grad = jnp.einsum(
        "bhqk,bqhd->bkhd", probs_low, context_grad, preferred_element_type=F32
    ).astype(BF)
    balance = jnp.sum(attention_probs * weight_grad, axis=-1, keepdims=True)
    score_grad = (attention_probs * (weight_grad - balance)).astype(BF)
    query_grad = (
        jnp.einsum("bhqk,bkhd->bqhd", score_grad, key_rows, preferred_element_type=F32) * score_scale
    ).astype(BF)
    key_grad = (
        jnp.einsum("bhqk,bqhd->bkhd", score_grad, queries, preferred_element_type=F32) * score_scale
    ).astype(BF)
    heads_bias_part = jnp.concatenate(
        [
            jnp.sum(query_grad, axis=(0, 1), dtype=F32),
            jnp.sum(value_grad, axis=(0, 1), dtype=F32),
        ],
        axis=1,
    )
    packed_grad = jnp.stack([query_grad, key_grad, value_grad], axis=3).reshape(
        rows, head_count * 3 * head_size
    )
    shrink_sum = (shrink_low.astype(F32) + shrink_got.astype(F32))[None]
    expand_sum = (expand_low.astype(F32) + expand_got.astype(F32))[None]
    heads_part = dot(packed_grad, first_low, (0, 0))
    merge_part = dot(context, attended_grad, (0, 0))
    dense_sum = sum_dense(jnp.concatenate([heads_part, merge_part], axis=0))
    heads_sum = dense_sum[: packed_grad.shape[1]].T
    merge_sum = dense_sum[packed_grad.shape[1] :]

    first_send = dot(rows_of(packed_grad, 1 - c), heads_weight, (1, 1), BF)
    first_got = core_swap(first_send).astype(F32)
    first_low_sum = (dot(rows_of(packed_grad, c), heads_weight, (1, 1)) + first_got).astype(BF)
    first_grad = first_low_sum.astype(F32) + side_swap(first_low_sum).astype(F32)
    first_gain_part = jnp.sum(first_grad * unit_one, axis=0)
    first_shift_part = jnp.sum(first_grad, axis=0)
    input_half = mixed_grad + norm_back(first_grad, unit_one, scale_one, gain_one)
    input_pair = core_swap(input_half)
    input_gradient = both_halves(input_half, input_pair)

    count = 5 + experts
    lines = up_to(count + 3, 8)
    line = np.arange(lines)[:, None]
    head_row = jnp.pad(heads_bias_part.reshape(-1), (0, width - heads_bias_part.size))
    vectors = (
        first_gain_part,
        first_shift_part,
        merge_bias_part,
        second_gain_part,
        second_shift_part,
    )
    shared = jnp.pad(router_part, ((5, lines - count), (0, 0)))
    for k, vector in enumerate(vectors):
        shared = shared + jnp.where(line == k, vector[None, :], 0.0)
    shared = shared + jnp.where(line == count, slot_bias_part[None, :], 0.0)
    sent_small = shared + jnp.where(line == count + 1, expand_bias_part[None, hidden_here:], 0.0)
    small = shared + jnp.where(line == count + 1, expand_bias_part[None, :hidden_here], 0.0)
    small = small + jnp.where(line == count + 2, head_row[None, :], 0.0)
    small = small + core_swap(sent_small)
    over_experts = (line < count) | (line == count + 2)
    n = lax.axis_size(EXPERT)
    step = 1
    while step < n:
        got = swap(small, EXPERT, step)
        small = small + jnp.where(over_experts, got, 0.0)
        step *= 2
    small = small + half_swap(small)
    heads_bias_sum = small[count + 2, : heads_bias_part.size].reshape(heads_bias_part.shape)
    return (
        outputs,
        input_gradient,
        small[0],
        small[1],
        heads_sum,
        heads_bias_sum,
        merge_sum,
        small[2],
        small[3],
        small[4],
        small[5:count].T,
        expand_sum,
        small[None, count + 1],
        shrink_sum,
        small[None, count],
    )


def solution(mesh):
    placed = (
        P((DP, EXPERT), None, None),
        P(),
        P(),
        P(None, TENSOR),
        P(TENSOR, None),
        P(TENSOR, None),
        P(),
        P(),
        P(),
        P(),
        P(EXPERT, None, TENSOR),
        P(EXPERT, TENSOR),
        P(EXPERT, TENSOR, None),
        P(EXPERT, None),
        P((DP, EXPERT), None, None),
        P((DP, EXPERT), None, None),
        P((DP, EXPERT), None, None),
        P((DP, EXPERT), None, None),
    )
    return jax.shard_map(
        whole_block,
        mesh=mesh,
        in_specs=placed,
        out_specs=(
            P((DP, EXPERT), None, None),
            P((DP, EXPERT), None, None),
            P(),
            P(),
            P(None, TENSOR),
            P(TENSOR, None),
            P(TENSOR, None),
            P(),
            P(),
            P(),
            P(),
            P(EXPERT, None, TENSOR),
            P(EXPERT, TENSOR),
            P(EXPERT, TENSOR, None),
            P(EXPERT, None),
        ),
        check_vma=False,
    )
```
